32 devices in a mesh: parts: 2 (over x), tile: 16 (over z, y, core).
Axes of the slice: x: 2, y: 2, z: 4, core: 2. Of those that a mesh axis runs over, the one named last changes fastest.
Arguments:
- src_slots: bfloat16 [32, 512, 512], P(('parts', 'tile')), parts along dimension 0, may hold values from -6 to 6
- v_tiles: bfloat16 [32, 16, 512, 256], P(('parts', 'tile')), parts along dimension 0, may hold values from -0.1875 to 0.1875
- u_tiles: bfloat16 [32, 16, 256, 512], P(('parts', 'tile')), parts along dimension 0, may hold values from -0.125 to 0.125
- ranks: int32 [2, 16, 16], P('parts'), parts along dimension 0, may hold values from 16 to 128, as said below
- col_map: int32 [2, 16], P('parts'), parts along dimension 0, may hold values from 0 to 15, each once within a row
- gate_start: int32 [32, 512], P('parts', 'tile'), parts along dimension 0, may hold values from 0 to 960
Outputs:
- image: bfloat16 [32, 512, 64, 256], P('parts', 'tile'), parts along dimension 0
The draws below stay inside these ranges and needn't reach their ends.
There are 2 independent parts, one for each index of `parts`. The reference program is written for one: setup_inputs(seed, part) draws one part's arguments, and reference() takes and returns one part's arrays. A program takes and returns all parts, laid end to end along the dimension named above; each array names one. Nothing has to cross between parts.
Inputs may be any that keep to these rules, and one draw needn't show every extreme that they name: `ranks`: each rank is a multiple of 16; the columns of V and U from a tile's rank on are not part of the tile. `col_map`: each row f is a permutation of the tile columns.
All inputs are finite; a program needn't handle non-finite values.
Results may differ from the reference program's by a relative error of at most 0.008.
Values may be sent and summed in bfloat16 or wider, within the bound.
No kernel may reach another device: no remote copies, remote signals or barrier semaphores. Data moves between devices by JAX's collectives and lax.ppermute only.
A program may use at most 192 MiB of HBM per device.

```python
import math
import jax
import jax.numpy as jnp
from jax import lax

B = 512
TC = 16
TR = 16
RMAX = 128
SIDE = 16
NT = 1024
GT = 64
S = 256
FW = 1
NK = 1
RB = 128


def draw_ranks(key, part):
    key_base = jax.random.fold_in(key, 11)
    key_heavy = jax.random.fold_in(key, 23)
    base_blocks = jax.random.randint(key_base, (FW, TR, TC), 1, max(2, RMAX // 32 + 1))
    heavy_tiles = jax.random.randint(key_heavy, (FW, TR, TC), 0, 8) == 0
    return (jnp.where(heavy_tiles, RMAX // 16, base_blocks) * 16).astype(jnp.int32)


def plant(entries, stream_key, least, top_value):
    index_at = [jax.random.randint(jax.random.fold_in(stream_key, axis), (), 0, length) for axis, length in enumerate(entries.shape)]
    widest = entries.shape.index(max(entries.shape))
    neighbour = index_at[:widest] + [(index_at[widest] + 1) % entries.shape[widest]] + index_at[widest + 1:]
    return entries.at[tuple(index_at)].set(least).at[tuple(neighbour)].set(top_value)


def level_of(own_key, extent, cuts, smallest, high):
    def one(axis_at, shards_of):
        steps = jax.random.uniform(jax.random.fold_in(jax.random.fold_in(own_key, 6), axis_at), (shards_of,), jnp.float32, smallest / len(cuts), high / len(cuts))
        return jnp.repeat(jnp.exp(steps), extent[axis_at] // shards_of).reshape((-1,) + (1,) * (len(extent) - axis_at - 1))

    loudness = one(*cuts[0])
    for cut in cuts[1:]:
        loudness = loudness * one(*cut)
    return loudness


def normal_values(stream_key, extent, deviation, most, split=(), kind=jnp.bfloat16):
    values = deviation * jax.random.normal(stream_key, extent, jnp.float32)
    if split:
        values = values * level_of(stream_key, extent, split, -0.22, 0.18)
    return jnp.clip(values, -most, most).astype(kind)


def setup_inputs(seed: int = 0, part: int = 0) -> dict:
    seeds = jax.random.split(jax.random.key(seed), 7)
    part_keys = jax.random.split(jax.random.fold_in(seeds[6], part), 7)
    src_slots = normal_values(part_keys[0], (FW * TC, B, 2 * S), 1.0, 6.0, ((0, 16),))
    v_tiles = normal_values(part_keys[1], (FW * TC, TR, B, 2 * RMAX), (2 * B) ** -0.5, 0.1875, ((0, 16),))
    u_tiles = normal_values(part_keys[2], (TR * NK, FW * TC, 2 * RB, B), (TC * RMAX) ** -0.5, 0.125, ((0, 16),))
    ranks = draw_ranks(jax.random.fold_in(jax.random.fold_in(seeds[6], part), 71), part)
    col_map = jax.vmap(lambda own: jax.random.permutation(own, TC))(jax.random.split(part_keys[4], FW)).reshape((FW, TC)).astype(jnp.int32)
    gate_start = plant(jax.random.randint(part_keys[5], (TR, B), 0, NT - GT + 1), jax.random.fold_in(part_keys[5], 1), 0, NT - GT).astype(jnp.int32)
    return dict(src_slots=src_slots, v_tiles=v_tiles, u_tiles=u_tiles, ranks=ranks, col_map=col_map, gate_start=gate_start)


edge_weight = 0.15
centre_weight = 0.7

def gated_trace(real_part, imag_part, gate_start, freq_count, samples, gate_len):
    sample_times = gate_start[:, :, None] + jnp.arange(gate_len, dtype=jnp.int32)[None, None, :]
    bin_index = 4 + jnp.arange(freq_count, dtype=jnp.int32) * (samples // (2 * freq_count))
    phases = bin_index[:, None, None, None] * sample_times[None] % samples
    angles = phases.astype(jnp.float32) * (2.0 * math.pi / samples)
    summed = jnp.einsum('firs,firt->irts', real_part, jnp.cos(angles), precision=lax.Precision.HIGHEST)
    summed = summed - jnp.einsum('firs,firt->irts', imag_part, jnp.sin(angles), precision=lax.Precision.HIGHEST)
    return summed * (2.0 / math.sqrt(freq_count))

def smooth_grid(signal, grid_side):
    grid_width = signal.shape[-1]
    column = jnp.arange(grid_width) % grid_side
    zeros_one = jnp.zeros(signal.shape[:-1] + (1,), signal.dtype)
    before = jnp.concatenate([zeros_one, signal[..., :-1]], axis=-1)
    before = jnp.where(column == 0, 0.0, before)
    after = jnp.concatenate([signal[..., 1:], zeros_one], axis=-1)
    after = jnp.where(column == grid_side - 1, 0.0, after)
    across = centre_weight * signal + edge_weight * (before + after)
    zeros_row = jnp.zeros(signal.shape[:-1] + (grid_side,), signal.dtype)
    above = jnp.concatenate([zeros_row, across[..., :-grid_side]], axis=-1)
    below = jnp.concatenate([across[..., grid_side:], zeros_row], axis=-1)
    return centre_weight * across + edge_weight * (above + below)

def reference(src_slots, v_tiles, u_tiles, ranks, col_map, gate_start):
    column_ids = jnp.arange(TC, dtype=jnp.int32)
    held_rank = lax.optimization_barrier(jnp.sum(jnp.where(col_map[:, :, None, None] == column_ids[None, None, None, :], ranks[:, None, :, :], 0), axis=-1))
    one_hot = (col_map[:, :, None] == column_ids[None, None, :]).astype(jnp.float32)

    def one_freq(freq_index):
        start = (freq_index * TC).astype(jnp.int32)
        tile_slots = lax.dynamic_slice_in_dim(v_tiles, start, TC, 0)
        sources = lax.dynamic_slice_in_dim(src_slots, start, TC, 0)
        product = jnp.einsum('xibr,xbs->xirs', tile_slots.astype(jnp.float32), sources.astype(jnp.float32))
        real_z = product[:, :, :RMAX, :S] - product[:, :, RMAX:, S:]
        imag_z = product[:, :, :RMAX, S:] + product[:, :, RMAX:, :S]
        rank_here = lax.dynamic_index_in_dim(held_rank, freq_index, 0, keepdims=False)
        live_rows = jnp.arange(RMAX, dtype=jnp.int32)[None, None, :, None] < rank_here[:, :, None, None]
        blocks = jnp.where(live_rows, jnp.concatenate([real_z, imag_z], axis=-1), 0.0).astype(jnp.bfloat16)
        mapping = lax.dynamic_index_in_dim(one_hot, freq_index, 0, keepdims=False)
        by_column = jnp.einsum('xj,xirs->jirs', mapping, blocks.astype(jnp.float32)).astype(jnp.bfloat16)
        by_column = by_column.reshape(TC, TR, NK, RB, 2 * S)
        swapped = jnp.concatenate([-by_column[..., S:], by_column[..., :S]], axis=-1)
        stacked = jnp.concatenate([by_column, swapped], axis=3)
        weights = lax.dynamic_slice_in_dim(u_tiles, start, TC, 1).reshape(TR, NK, TC, 2 * RB, B)
        partial_value = jnp.einsum('ikjcb,jikcs->ikbs', weights.astype(jnp.float32), stacked.astype(jnp.float32)).astype(jnp.bfloat16)
        return lax.optimization_barrier(jnp.sum(partial_value.astype(jnp.float32), axis=1))
    spectrum = lax.map(one_freq, jnp.arange(FW, dtype=jnp.int32))
    traces = gated_trace(spectrum[..., :S], spectrum[..., S:], gate_start, FW, NT, GT)
    return smooth_grid(traces, SIDE).astype(jnp.bfloat16)
```

```python
import functools
import math

import jax
import jax.numpy as jnp
from jax import lax
from jax.experimental import pallas as pl
from jax.experimental.pallas import tpu as pltpu
from jax.sharding import PartitionSpec as P

TC = 16
TR = 16
RMAX = 128
SIDE = 16
NT = 1024
GT = 64

edge_weight = 0.15
centre_weight = 0.7


def over_rows(left, right):
    return lax.dot_general(
        left, right, (((0,), (0,)), ((), ())), preferred_element_type=jnp.float32
    )


def project_kernel(rank_ref, v_ref, x_ref, z_ref):
    tiles = v_ref.shape[0]
    sources = x_ref.shape[-1] // 2
    first = pl.program_id(0) * tiles
    row = lax.broadcasted_iota(jnp.int32, (RMAX, 2 * sources), 0)
    for t in range(tiles):
        product = over_rows(v_ref[t], x_ref[0])
        real_z = product[:RMAX, :sources] - product[RMAX:, sources:]
        imag_z = product[:RMAX, sources:] + product[RMAX:, :sources]
        both = jnp.concatenate([real_z, imag_z], axis=-1)
        z_ref[t] = jnp.where(row < rank_ref[first + t], both, 0.0).astype(jnp.bfloat16)


def project(rank_rows, v_tiles, src_slots, tiles):
    _, rows, tile_len, wide = v_tiles.shape
    cols = src_slots.shape[-1]
    return pl.pallas_call(
        project_kernel,
        out_shape=jax.ShapeDtypeStruct((rows, RMAX, cols), jnp.bfloat16),
        grid_spec=pltpu.PrefetchScalarGridSpec(
            num_scalar_prefetch=1,
            grid=(rows // tiles,),
            in_specs=[
                pl.BlockSpec((None, tiles, tile_len, wide), lambda i, r: (0, i, 0, 0)),
                pl.BlockSpec((1, tile_len, cols), lambda i, r: (0, 0, 0)),
            ],
            out_specs=pl.BlockSpec((tiles, RMAX, cols), lambda i, r: (i, 0, 0)),
        ),
        name="project",
    )(rank_rows, v_tiles, src_slots)


def expand_kernel(col_ref, z_ref, u_ref, y_ref, acc_ref):
    f = pl.program_id(0)
    sources = z_ref.shape[-1] // 2
    for x in range(TC):
        z = z_ref[x]
        swapped = jnp.concatenate([-z[:, sources:], z[:, :sources]], axis=-1)
        stacked = jnp.concatenate([z, swapped], axis=0)
        term = over_rows(u_ref[col_ref[f, x]], stacked)
        if x == 0:
            acc_ref[...] = term
        else:
            acc_ref[...] += term
    y_ref[...] = acc_ref[...].astype(jnp.bfloat16)


def expand(col_map, incoming, u_tiles):
    freq_count = col_map.shape[0]
    _, rank_block, cols = incoming.shape
    tile_len = u_tiles.shape[-1]
    incoming = incoming.reshape(freq_count, TC, rank_block, cols)
    weights = u_tiles.reshape(freq_count, TC, 2 * rank_block, tile_len)
    return pl.pallas_call(
        expand_kernel,
        out_shape=jax.ShapeDtypeStruct((freq_count, tile_len, cols), jnp.bfloat16),
        grid_spec=pltpu.PrefetchScalarGridSpec(
            num_scalar_prefetch=1,
            grid=(freq_count,),
            in_specs=[
                pl.BlockSpec((None, TC, rank_block, cols), lambda f, c: (f, 0, 0, 0)),
                pl.BlockSpec((None, TC, 2 * rank_block, tile_len), lambda f, c: (f, 0, 0, 0)),
            ],
            out_specs=pl.BlockSpec((None, tile_len, cols), lambda f, c: (f, 0, 0)),
            scratch_shapes=[pltpu.VMEM((tile_len, cols), jnp.float32)],
        ),
        name="expand",
    )(col_map, incoming, weights)


def smooth(signal):
    width = signal.shape[-1]
    place = lax.broadcasted_iota(jnp.int32, signal.shape, 1)
    column = place % SIDE
    before = jnp.where(column == 0, 0.0, pltpu.roll(signal, 1, axis=1))
    after = jnp.where(column == SIDE - 1, 0.0, pltpu.roll(signal, width - 1, axis=1))
    across = centre_weight * signal + edge_weight * (before + after)
    above = jnp.where(place < SIDE, 0.0, pltpu.roll(across, SIDE, axis=1))
    below = jnp.where(place >= width - SIDE, 0.0, pltpu.roll(across, width - SIDE, axis=1))
    return centre_weight * across + edge_weight * (above + below)


def gate_kernel(y_ref, cos_g_ref, sin_g_ref, cos_t_ref, sin_t_ref, out_ref, a_ref, b_ref):
    freq_count, blocks, receivers, cols = y_ref.shape
    sources = cols // 2
    lanes = cos_t_ref.shape[-1]
    for f in range(freq_count):
        summed = y_ref[f, 0].astype(jnp.float32)
        for k in range(1, blocks):
            summed = summed + y_ref[f, k].astype(jnp.float32)
        real_y = smooth(summed[:, :sources])
        imag_y = smooth(summed[:, sources:])
        cos_g = cos_g_ref[f]
        sin_g = sin_g_ref[f]
        a_ref[f] = cos_g * real_y - sin_g * imag_y
        b_ref[f] = sin_g * real_y + cos_g * imag_y

    for r in range(receivers):
        for start in range(0, sources, lanes):
            total = None
            for f in range(freq_count):
                a = a_ref[f, r:r + 1, start:start + lanes]
                b = b_ref[f, r:r + 1, start:start + lanes]
                term = cos_t_ref[f] * a - sin_t_ref[f] * b
                total = term if total is None else total + term
            out_ref[r, :, start:start + lanes] = total.astype(out_ref.dtype)


def gate(arrived, cos_g, sin_g, cos_t, sin_t):
    freq_count, rows, blocks, receivers, cols = arrived.shape
    sources = cols // 2
    gate_len, lanes = cos_t.shape[1:]
    whole = lambda i: (0, 0, 0)
    return pl.pallas_call(
        gate_kernel,
        out_shape=jax.ShapeDtypeStruct((rows, receivers, gate_len, sources), jnp.bfloat16),
        grid=(rows,),
        in_specs=[
            pl.BlockSpec((freq_count, None, blocks, receivers, cols), lambda i: (0, i, 0, 0, 0)),
            pl.BlockSpec((freq_count, None, receivers, 1), lambda i: (0, i, 0, 0)),
            pl.BlockSpec((freq_count, None, receivers, 1), lambda i: (0, i, 0, 0)),
            pl.BlockSpec((freq_count, gate_len, lanes), whole),
            pl.BlockSpec((freq_count, gate_len, lanes), whole),
        ],
        out_specs=pl.BlockSpec((None, receivers, gate_len, sources), lambda i: (i, 0, 0, 0)),
        scratch_shapes=[pltpu.VMEM((freq_count, receivers, sources), jnp.float32)] * 2,
        name="gate",
    )(arrived, cos_g, sin_g, cos_t, sin_t)


def waves(times, bins):
    phases = bins.reshape((-1,) + (1,) * times.ndim) * times[None] % NT
    angles = phases.astype(jnp.float32) * (2.0 * math.pi / NT)
    return jnp.cos(angles), jnp.sin(angles)


def on_device(src_slots, v_tiles, u_tiles, ranks, col_map, gate_start):
    devices = lax.axis_size("tile")
    device = lax.axis_index("tile")
    freq_count = devices // TC
    blocks_per = devices // TR
    rank_block = RMAX // blocks_per
    cols = src_slots.shape[-1]
    tile_len = v_tiles.shape[2]
    receivers = tile_len // devices
    column_ids = jnp.arange(TC, dtype=jnp.int32)
    freq_ids = jnp.arange(freq_count, dtype=jnp.int32)
    slot_rows = (freq_ids[:, None] == device // TC) & (column_ids[None, :] == device % TC)
    mine = jnp.sum(
        jnp.where(slot_rows[:, :, None] & (col_map[:, :, None] == column_ids), 1, 0), axis=1
    )
    rank_rows = jnp.sum(ranks * mine[:, None, :], axis=(0, 2))

    reduced = project(rank_rows, v_tiles, src_slots, 2)
    outgoing = reduced.reshape(devices, rank_block, cols)
    incoming = lax.all_to_all(outgoing, "tile", split_axis=0, concat_axis=0, tiled=True)
    partial_value = expand(col_map, incoming, u_tiles)
    spread = partial_value.reshape(freq_count, devices, receivers, cols)
    arrived = lax.all_to_all(spread, "tile", split_axis=1, concat_axis=1, tiled=True)
    arrived = arrived.reshape(freq_count, TR, blocks_per, receivers, cols)

    bins = 4 + freq_ids * (NT // (2 * freq_count))
    scale = 2.0 / math.sqrt(freq_count)
    cos_g, sin_g = waves(gate_start, bins)
    cos_t, sin_t = waves(jnp.arange(GT, dtype=jnp.int32), bins)
    lanes = min(128, cols // 2)
    cos_t, sin_t = (
        jnp.broadcast_to(wave[:, :, None], wave.shape + (lanes,)) for wave in (cos_t, sin_t)
    )
    return gate(arrived, scale * cos_g[..., None], scale * sin_g[..., None], cos_t, sin_t)


def solution(mesh):
    placed = (
        P(("parts", "tile"), None, None),
        P(("parts", "tile"), None, None, None),
        P(("parts", "tile"), None, None, None),
        P("parts", None, None),
        P("parts", None),
        P("parts", "tile"),
    )
    return jax.shard_map(
        on_device,
        mesh=mesh,
        in_specs=placed,
        out_specs=P("parts", "tile", None, None),
        check_vma=False,
    )
```

```python
import math

import jax
import jax.numpy as jnp
from jax import lax
from jax.experimental import pallas as pl
from jax.experimental.pallas import tpu as pltpu
from jax.sharding import PartitionSpec as P

TC = 16
TR = 16
RMAX = 128
SIDE = 16
NT = 1024
GT = 64

edge_weight = 0.15
centre_weight = 0.7


def matmul(left, right, left_dim=1):
    return lax.dot_general(
        left, right, (((left_dim,), (0,)), ((), ())), preferred_element_type=jnp.float32
    )


def project_kernel(turned, rank_ref, col_ref, v_ref, x_ref, z_ref, left_ref):
    tiles, tile_len, _ = v_ref.shape
    sources = x_ref.shape[-1] // 2
    device = lax.axis_index("tile")
    freq, slot = device // TC, device % TC
    column = col_ref[freq, slot]

    @pl.when(pl.program_id(0) == 0)
    def _():
        real_x = x_ref[0, :, :sources].T
        imag_x = x_ref[0, :, sources:].T
        left_ref[:sources, :tile_len] = real_x
        left_ref[:sources, tile_len:] = -imag_x
        left_ref[sources:, :tile_len] = imag_x
        left_ref[sources:, tile_len:] = real_x

    first = pl.program_id(0) * tiles
    lane = lax.broadcasted_iota(jnp.int32, (1, 2 * RMAX), 1)
    for t in range(0, tiles, 2):
        one, two = v_ref[t], v_ref[t + 1]
        real_v = jnp.concatenate([one[:, :RMAX], two[:, :RMAX]], axis=1)
        imag_v = jnp.concatenate([one[:, RMAX:], two[:, RMAX:]], axis=1)
        both = matmul(left_ref[...], jnp.concatenate([real_v, imag_v], axis=0))
        rank_one = rank_ref[freq, first + t, column]
        rank_two = rank_ref[freq, first + t + 1, column] + RMAX
        live = (lane < rank_one) | ((lane >= RMAX) & (lane < rank_two))
        both = jnp.where(live, both, 0.0).astype(jnp.bfloat16)
        for side in range(2):
            z = both[:, side * RMAX:(side + 1) * RMAX]
            z_ref[t + side] = z if turned else z.T


def project(ranks, col_map, v_tiles, src_slots, tiles, turned):
    _, rows, tile_len, wide = v_tiles.shape
    cols = src_slots.shape[-1]
    shape = (cols, RMAX) if turned else (RMAX, cols)
    return pl.pallas_call(
        lambda *refs: project_kernel(turned, *refs),
        out_shape=jax.ShapeDtypeStruct((rows,) + shape, jnp.bfloat16),
        grid=(rows // tiles,),
        in_specs=[
            pl.BlockSpec(memory_space=pltpu.SMEM),
            pl.BlockSpec(memory_space=pltpu.SMEM),
            pl.BlockSpec((None, tiles, tile_len, wide), lambda i: (0, i, 0, 0)),
            pl.BlockSpec((1, tile_len, cols), lambda i: (0, 0, 0)),
        ],
        out_specs=pl.BlockSpec((tiles,) + shape, lambda i: (i, 0, 0)),
        scratch_shapes=[pltpu.VMEM((cols, 2 * tile_len), jnp.bfloat16)],
        name="project",
    )(ranks, col_map, v_tiles, src_slots)


def expand_kernel(turned, col_ref, z_ref, u_ref, y_ref, acc_ref):
    freq_count = u_ref.shape[0]
    sources = y_ref.shape[-1] // 2
    for f in range(freq_count):
        for x in range(TC):
            z = z_ref[f, x]
            if turned:
                real_z, imag_z = z[:sources], z[sources:]
                upper = jnp.concatenate([real_z, -imag_z], axis=1)
                lower = jnp.concatenate([imag_z, real_z], axis=1)
                left = jnp.concatenate([upper, lower], axis=0)
            else:
                real_z, imag_z = z[:, :sources], z[:, sources:]
                upper = jnp.concatenate([real_z, imag_z], axis=1)
                lower = jnp.concatenate([-imag_z, real_z], axis=1)
                left = jnp.concatenate([upper, lower], axis=0)
            term = matmul(left, u_ref[f, col_ref[f, x]], 1 if turned else 0)
            if x == 0:
                acc_ref[...] = term
            else:
                acc_ref[...] += term
        y_ref[f] = acc_ref[...].astype(jnp.bfloat16).T


def expand(col_map, incoming, u_tiles, cols, turned):
    freq_count = col_map.shape[0]
    rank_block = incoming.shape[-1] if turned else incoming.shape[-2]
    tile_len = u_tiles.shape[-1]
    incoming = incoming.reshape((freq_count, TC) + incoming.shape[1:])
    weights = u_tiles.reshape(freq_count, TC, 2 * rank_block, tile_len)
    return pl.pallas_call(
        lambda *refs: expand_kernel(turned, *refs),
        out_shape=jax.ShapeDtypeStruct((freq_count, tile_len, cols), jnp.bfloat16),
        in_specs=[
            pl.BlockSpec(memory_space=pltpu.SMEM),
            pl.BlockSpec(memory_space=pltpu.VMEM),
            pl.BlockSpec(memory_space=pltpu.VMEM),
        ],
        out_specs=pl.BlockSpec(memory_space=pltpu.VMEM),
        scratch_shapes=[pltpu.VMEM((cols, tile_len), jnp.float32)],
        compiler_params=pltpu.CompilerParams(vmem_limit_bytes=24 * 2**20),
        name="expand",
    )(col_map, incoming, weights)


def split(value):
    high = value.astype(jnp.bfloat16)
    return high, (value - high.astype(jnp.float32)).astype(jnp.bfloat16)


def smoother(sources):
    place = jnp.arange(sources, dtype=jnp.int32)
    row, column = place // SIDE, place % SIDE

    def one(at):
        apart = jnp.abs(at[:, None] - at[None, :])
        return jnp.where(apart == 0, centre_weight, jnp.where(apart == 1, edge_weight, 0.0))

    return jnp.concatenate(split(one(row) * one(column)), axis=0)


def mix_rows(y_ref, cos_g_ref, sin_g_ref, smooth_ref, mix_ref, first, count):
    freq_count, _, blocks, receivers, cols = y_ref.shape
    sources = cols // 2
    many = count * receivers
    for f in range(freq_count):
        if blocks == 1:
            parts = [y_ref[f, first:first + count, 0]]
        else:
            summed = y_ref[f, first:first + count, 0].astype(jnp.float32)
            for k in range(1, blocks):
                summed = summed + y_ref[f, first:first + count, k].astype(jnp.float32)
            parts = split(summed)
        smoothed = None
        for part in parts:
            part = part.reshape(many, cols)
            left = jnp.concatenate([part[:, :sources], part[:, sources:]], axis=0)
            term = matmul(jnp.concatenate([left, left], axis=1), smooth_ref[...])
            smoothed = term if smoothed is None else smoothed + term
        real_y, imag_y = smoothed[:many], smoothed[many:]
        cos_g = cos_g_ref[f, first:first + count].reshape(many, 1)
        sin_g = sin_g_ref[f, first:first + count].reshape(many, 1)
        shape = (count, receivers, sources)
        mix_ref[f, 0, first:first + count] = (cos_g * real_y - sin_g * imag_y).reshape(shape)
        mix_ref[f, 1, first:first + count] = (sin_g * real_y + cos_g * imag_y).reshape(shape)


def gate_kernel(y_ref, cos_g_ref, sin_g_ref, smooth_ref, wave_ref, out_ref, mix_ref):
    rows, receivers, gate_len, sources = out_ref.shape
    freq_count, all_rows = y_ref.shape[:2]
    high = 16

    @pl.when(pl.program_id(0) == 0)
    def _():
        for first in range(0, all_rows, 4):
            mix_rows(y_ref, cos_g_ref, sin_g_ref, smooth_ref, mix_ref, first, 4)

    for i in range(rows):
        row = pl.program_id(0) * rows + i
        for r in range(receivers):
            mixed = [
                [
                    jnp.broadcast_to(mix_ref[f, p, row, r:r + 1], (high, sources)).astype(
                        jnp.bfloat16
                    )
                    for p in range(2)
                ]
                for f in range(freq_count)
            ]
            for top in range(0, gate_len, high):
                down = slice(top, top + high)
                terms = [
                    wave_ref[f, 0, down] * mixed[f][0] - wave_ref[f, 1, down] * mixed[f][1]
                    for f in range(freq_count)
                ]
                total = terms[0]
                if freq_count > 1:
                    total = sum(term.astype(jnp.float32) for term in terms)
                out_ref[i, r, down] = total.astype(out_ref.dtype)


def gate(arrived, cos_g, sin_g, smooth, wave, step):
    freq_count, rows, _, receivers, cols = arrived.shape
    sources = cols // 2
    gate_len = wave.shape[2]
    return pl.pallas_call(
        gate_kernel,
        out_shape=jax.ShapeDtypeStruct((rows, receivers, gate_len, sources), jnp.bfloat16),
        grid=(rows // step,),
        in_specs=[pl.BlockSpec(memory_space=pltpu.VMEM)] * 5,
        out_specs=pl.BlockSpec((step, receivers, gate_len, sources), lambda i: (i, 0, 0, 0)),
        scratch_shapes=[pltpu.VMEM((freq_count, 2, rows, receivers, sources), jnp.float32)],
        compiler_params=pltpu.CompilerParams(vmem_limit_bytes=32 * 2**20),
        name="gate",
    )(arrived, cos_g, sin_g, smooth, wave)


def waves(times, bins):
    phases = bins.reshape((-1,) + (1,) * times.ndim) * times[None] % NT
    angles = phases.astype(jnp.float32) * (2.0 * math.pi / NT)
    return jnp.cos(angles), jnp.sin(angles)


def gate_waves(bins, lanes):
    both = jnp.stack(waves(jnp.arange(GT, dtype=jnp.int32), bins), axis=1).astype(jnp.bfloat16)
    return jnp.broadcast_to(both[..., None], both.shape + (lanes,))


def on_device(src_slots, v_tiles, u_tiles, ranks, col_map, gate_start):
    devices = lax.axis_size("tile")
    freq_count = devices // TC
    blocks_per = devices // TR
    rank_block = RMAX // blocks_per
    turned = rank_block == RMAX
    cols = src_slots.shape[-1]
    tile_len = v_tiles.shape[2]
    receivers = tile_len // devices
    freq_ids = jnp.arange(freq_count, dtype=jnp.int32)

    outgoing = project(ranks, col_map, v_tiles, src_slots, 4, turned)
    if not turned:
        outgoing = outgoing.reshape(devices, rank_block, cols)
    incoming = lax.all_to_all(outgoing, "tile", split_axis=0, concat_axis=0, tiled=True)
    partial_value = expand(col_map, incoming, u_tiles, cols, turned)
    spread = partial_value.reshape(freq_count, devices, receivers, cols)
    arrived = lax.all_to_all(spread, "tile", split_axis=1, concat_axis=1, tiled=True)
    arrived = arrived.reshape(freq_count, TR, blocks_per, receivers, cols)

    bins = 4 + freq_ids * (NT // (2 * freq_count))
    scale = 2.0 / math.sqrt(freq_count)
    cos_g, sin_g = waves(gate_start, bins)
    cos_g, sin_g = scale * cos_g[..., None], scale * sin_g[..., None]
    wave = gate_waves(bins, cols // 2)
    return gate(arrived, cos_g, sin_g, smoother(cols // 2), wave, 2)


def solution(mesh):
    placed = (
        P(("parts", "tile"), None, None),
        P(("parts", "tile"), None, None, None),
        P(("parts", "tile"), None, None, None),
        P("parts", None, None),
        P("parts", None),
        P("parts", "tile"),
    )
    return jax.shard_map(
        on_device,
        mesh=mesh,
        in_specs=placed,
        out_specs=P("parts", "tile", None, None),
        check_vma=False,
    )
```

```python
import functools
import math

import jax
import jax.numpy as jnp
from jax import lax
from jax.experimental import pallas as pl
from jax.experimental.pallas import tpu as pltpu
from jax.sharding import PartitionSpec as P


TC = 16
TR = 16
RMAX = 128
SIDE = 16
NT = 1024
GT = 64
sends = (2, 6, 8)
takes = (8, 6, 2)


edge_weight = 0.15
centre_weight = 0.7


def matmul(left, right, left_dim=1):
    return lax.dot_general(
        left, right, (((left_dim,), (0,)), ((), ())), preferred_element_type=jnp.float32
    )


def project_kernel(turned, rank_ref, col_ref, v_ref, x_ref, z_ref, left_ref):
    tiles, tile_len, _ = v_ref.shape
    sources = x_ref.shape[-1] // 2
    device = lax.axis_index("tile")
    freq, slot = device // TC, device % TC
    column = col_ref[freq, slot]

    @pl.when(pl.program_id(0) == 0)
    def _():
        real_x = x_ref[0, :, :sources].T
        imag_x = x_ref[0, :, sources:].T
        left_ref[:sources, :tile_len] = real_x
        left_ref[:sources, tile_len:] = -imag_x
        left_ref[sources:, :tile_len] = imag_x
        left_ref[sources:, tile_len:] = real_x

    first = pl.program_id(0) * tiles
    lane = lax.broadcasted_iota(jnp.int32, (1, 2 * RMAX), 1)
    for t in range(0, tiles, 2):
        one, two = v_ref[t], v_ref[t + 1]
        real_v = jnp.concatenate([one[:, :RMAX], two[:, :RMAX]], axis=1)
        imag_v = jnp.concatenate([one[:, RMAX:], two[:, RMAX:]], axis=1)
        both = matmul(left_ref[...], jnp.concatenate([real_v, imag_v], axis=0))
        rank_one = rank_ref[freq, first + t, column]
        rank_two = rank_ref[freq, first + t + 1, column] + RMAX
        live = (lane < rank_one) | ((lane >= RMAX) & (lane < rank_two))
        both = jnp.where(live, both, 0.0).astype(jnp.bfloat16)
        for side in range(2):
            z = both[:, side * RMAX:(side + 1) * RMAX]
            z_ref[t + side] = z if turned else z.T


def project(ranks, col_map, v_tiles, src_slots, tiles, turned):
    _, rows, tile_len, wide = v_tiles.shape
    cols = src_slots.shape[-1]
    shape = (cols, RMAX) if turned else (RMAX, cols)
    return pl.pallas_call(
        lambda *refs: project_kernel(turned, *refs),
        out_shape=jax.ShapeDtypeStruct((rows,) + shape, jnp.bfloat16),
        grid=(rows // tiles,),
        in_specs=[
            pl.BlockSpec(memory_space=pltpu.SMEM),
            pl.BlockSpec(memory_space=pltpu.SMEM),
            pl.BlockSpec((None, tiles, tile_len, wide), lambda i: (0, i, 0, 0)),
            pl.BlockSpec((1, tile_len, cols), lambda i: (0, 0, 0)),
        ],
        out_specs=pl.BlockSpec((tiles,) + shape, lambda i: (i, 0, 0)),
        scratch_shapes=[pltpu.VMEM((cols, 2 * tile_len), jnp.bfloat16)],
        name="project",
    )(ranks, col_map, v_tiles, src_slots)


def expand_kernel(turned, col_ref, z_ref, u_ref, y_ref, acc_ref):
    freq_count = u_ref.shape[0]
    sources = y_ref.shape[-1] // 2
    for f in range(freq_count):
        for x in range(TC):
            z = z_ref[f, x]
            if turned:
                real_z, imag_z = z[:sources], z[sources:]
                upper = jnp.concatenate([real_z, -imag_z], axis=1)
                lower = jnp.concatenate([imag_z, real_z], axis=1)
                left = jnp.concatenate([upper, lower], axis=0)
            else:
                real_z, imag_z = z[:, :sources], z[:, sources:]
                upper = jnp.concatenate([real_z, imag_z], axis=1)
                lower = jnp.concatenate([-imag_z, real_z], axis=1)
                left = jnp.concatenate([upper, lower], axis=0)
            term = matmul(left, u_ref[f, col_ref[f, x]], 1 if turned else 0)
            if x == 0:
                acc_ref[...] = term
            else:
                acc_ref[...] += term
        y_ref[f] = acc_ref[...].astype(jnp.bfloat16).T


def expand(col_map, incoming, u_tiles, cols, turned):
    freq_count = col_map.shape[0]
    rank_block = incoming.shape[-1] if turned else incoming.shape[-2]
    tile_len = u_tiles.shape[-1]
    incoming = incoming.reshape((freq_count, TC) + incoming.shape[1:])
    weights = u_tiles.reshape(freq_count, TC, 2 * rank_block, tile_len)
    return pl.pallas_call(
        lambda *refs: expand_kernel(turned, *refs),
        out_shape=jax.ShapeDtypeStruct((freq_count, tile_len, cols), jnp.bfloat16),
        in_specs=[
            pl.BlockSpec(memory_space=pltpu.SMEM),
            pl.BlockSpec(memory_space=pltpu.VMEM),
            pl.BlockSpec(memory_space=pltpu.VMEM),
        ],
        out_specs=pl.BlockSpec(memory_space=pltpu.VMEM),
        scratch_shapes=[pltpu.VMEM((cols, tile_len), jnp.float32)],
        compiler_params=pltpu.CompilerParams(vmem_limit_bytes=24 * 2**20),
        name="expand",
    )(col_map, incoming, weights)


def far_first(devices):
    return sorted(range(1, devices), key=lambda k: (-(k >> 2), k)) + [0]


def send_first_kernel(ids, rank_hbm, col_hbm, v_hbm, x_hbm, *refs):
    count = len(ids)
    z_refs = refs[:count]
    left_ref, x_ref, tile_ref, rank_ref, col_ref, sems = refs[count:]
    device = lax.axis_index("tile")
    rows = [jnp.bitwise_xor(device, k) for k in ids]
    copies = [
        pltpu.make_async_copy(x_hbm.at[0], x_ref, sems.at[count]),
        pltpu.make_async_copy(rank_hbm.at[0], rank_ref, sems.at[count + 1]),
        pltpu.make_async_copy(col_hbm, col_ref, sems.at[count + 2]),
    ]
    for n, row in enumerate(rows):
        copies.append(pltpu.make_async_copy(v_hbm.at[0, row], tile_ref.at[n], sems.at[n]))
    for copy in copies:
        copy.start()
    copies[0].wait()
    build_left(x_ref[...], left_ref)
    for copy in copies[1:]:
        copy.wait()
    column = col_ref[0, device]
    for n in range(0, count, 2):
        tiles = [tile_ref[n], tile_ref[n + 1]]
        ranks = [rank_ref[rows[n], column], rank_ref[rows[n + 1], column]]
        z_refs[n][...], z_refs[n + 1][...] = project_two(left_ref, tiles, ranks)


def build_left(x, left_ref):
    tile_len, cols = x.shape
    sources = cols // 2
    real_x = x[:, :sources].T
    imag_x = x[:, sources:].T
    left_ref[:sources, :tile_len] = real_x
    left_ref[:sources, tile_len:] = -imag_x
    left_ref[sources:, :tile_len] = imag_x
    left_ref[sources:, tile_len:] = real_x


def send_kernel(ids, rank_ref, col_ref, v_ref, x_ref, *refs):
    z_refs, left_ref = refs[:-1], refs[-1]
    build_left(x_ref[0], left_ref)
    device = lax.axis_index("tile")
    column = col_ref[0, device]
    rows = [jnp.bitwise_xor(device, k) for k in ids]
    for n in range(0, len(ids), 2):
        tiles = [v_ref[0, rows[n]], v_ref[0, rows[n + 1]]]
        ranks = [rank_ref[0, rows[n], column], rank_ref[0, rows[n + 1], column]]
        z_refs[n][...], z_refs[n + 1][...] = project_two(left_ref, tiles, ranks)


def project_two(left_ref, tiles, ranks):
    lane = lax.broadcasted_iota(jnp.int32, (1, 2 * RMAX), 1)
    one, two = tiles
    real_v = jnp.concatenate([one[:, :RMAX], two[:, :RMAX]], axis=1)
    imag_v = jnp.concatenate([one[:, RMAX:], two[:, RMAX:]], axis=1)
    both = matmul(left_ref[...], jnp.concatenate([real_v, imag_v], axis=0))
    live = (lane < ranks[0]) | ((lane >= RMAX) & (lane < ranks[1] + RMAX))
    both = jnp.where(live, both, 0.0).astype(jnp.bfloat16)
    return both[:, :RMAX], both[:, RMAX:]


def send_tiles(ids, ranks, col_map, v_tiles, src_slots, first):
    tile_len, wide = v_tiles.shape[2:]
    cols = src_slots.shape[-1]
    count = len(ids)
    vmem, smem, hbm = (
        pl.BlockSpec(memory_space=m) for m in (pltpu.VMEM, pltpu.SMEM, pltpu.HBM)
    )
    left = pltpu.VMEM((cols, 2 * tile_len), jnp.bfloat16)
    scratch = [
        left,
        pltpu.VMEM((tile_len, cols), jnp.bfloat16),
        pltpu.VMEM((count, tile_len, wide), jnp.bfloat16),
        pltpu.SMEM(ranks.shape[1:], jnp.int32),
        pltpu.SMEM(col_map.shape, jnp.int32),
        pltpu.SemaphoreType.DMA((count + 3,)),
    ]
    return pl.pallas_call(
        functools.partial(send_first_kernel if first else send_kernel, ids),
        out_shape=[jax.ShapeDtypeStruct((cols, RMAX), jnp.bfloat16) for _ in ids],
        in_specs=[hbm] * 4 if first else [smem, smem, vmem, vmem],
        out_specs=[vmem] * count,
        scratch_shapes=scratch if first else [left],
        compiler_params=pltpu.CompilerParams(
            vmem_limit_bytes=(60 if first else 12) * 2**20
        ),
        cost_estimate=pl.CostEstimate(
            flops=2 * count * cols * 2 * tile_len * RMAX,
            bytes_accessed=count * tile_len * wide * 2,
            transcendentals=0,
        ),
        name="send_first" if first else "send_tiles",
    )(ranks, col_map, v_tiles, src_slots)


def add_kernel(ids, first, last, col_ref, u_ref, *refs):
    count = len(ids)
    z_refs, out_ref = refs[:count], refs[count if first else count + 1]
    total_ref = refs[-1]
    sources = z_refs[0].shape[0] // 2
    device = lax.axis_index("tile")
    for n, k in enumerate(ids):
        z = z_refs[n][...]
        real_z, imag_z = z[:sources], z[sources:]
        upper = jnp.concatenate([real_z, -imag_z], axis=1)
        lower = jnp.concatenate([imag_z, real_z], axis=1)
        left = jnp.concatenate([upper, lower], axis=0)
        term = matmul(left, u_ref[0, col_ref[0, jnp.bitwise_xor(device, k)]])
        if n == 0:
            total_ref[...] = term if first else refs[count][...] + term
        else:
            total_ref[...] += term
    if last:
        out_ref[0] = total_ref[...].astype(jnp.bfloat16).T
    else:
        out_ref[...] = total_ref[...]


def add_tiles(ids, tiles, col_map, u_tiles, total=None, last=False):
    first = total is None
    cols = tiles[0].shape[0]
    tile_len = u_tiles.shape[-1]
    vmem, smem = (pl.BlockSpec(memory_space=m) for m in (pltpu.VMEM, pltpu.SMEM))
    operands = [col_map, u_tiles, *tiles] + ([] if first else [total])
    shape = (
        jax.ShapeDtypeStruct((1, tile_len, cols), jnp.bfloat16)
        if last
        else jax.ShapeDtypeStruct((cols, tile_len), jnp.float32)
    )
    flops = 2 * len(ids) * cols * 2 * RMAX * tile_len
    return pl.pallas_call(
        lambda *refs: add_kernel(ids, first, last, *refs),
        out_shape=shape,
        in_specs=[smem] + [vmem] * (len(operands) - 1),
        out_specs=vmem,
        scratch_shapes=[pltpu.VMEM((cols, tile_len), jnp.float32)],
        compiler_params=pltpu.CompilerParams(vmem_limit_bytes=12 * 2**20),
        cost_estimate=pl.CostEstimate(
            flops=flops, bytes_accessed=len(ids) * cols * RMAX * 2, transcendentals=0
        ),
        name="add_tiles",
    )(*operands)


def far_last(devices):
    half = devices // 2
    return list(range(half)) + [k for k in far_first(devices) if k >= half]


def exchange(ranks, col_map, v_tiles, src_slots, u_tiles):
    devices = lax.axis_size("tile")
    arrived, at = {}, 0
    for group, count in enumerate(sends):
        ids = far_first(devices)[at:at + count]
        tiles = send_tiles(ids, ranks, col_map, v_tiles, src_slots, group == 0)
        for k, tile in zip(ids, tiles):
            arrived[k] = tile
            if k:
                pairs = [(d, d ^ k) for d in range(devices)]
                arrived[k] = lax.ppermute(tile, "tile", pairs)
        at += count
    total, at = None, 0
    for count in takes:
        ids = far_last(devices)[at:at + count]
        at += count
        total = add_tiles(
            ids, [arrived[k] for k in ids], col_map, u_tiles, total, at == devices
        )
    return total


def split(value):
    high = value.astype(jnp.bfloat16)
    return high, (value - high.astype(jnp.float32)).astype(jnp.bfloat16)


def smoother(sources):
    place = jnp.arange(sources, dtype=jnp.int32)
    row, column = place // SIDE, place % SIDE

    def one(at):
        apart = jnp.abs(at[:, None] - at[None, :])
        return jnp.where(apart == 0, centre_weight, jnp.where(apart == 1, edge_weight, 0.0))

    return jnp.concatenate(split(one(row) * one(column)), axis=0)


def mix_rows(y_ref, cos_g_ref, sin_g_ref, smooth_ref, mix_ref, first, count):
    freq_count, _, blocks, receivers, cols = y_ref.shape
    sources = cols // 2
    many = count * receivers
    for f in range(freq_count):
        if blocks == 1:
            parts = [y_ref[f, first:first + count, 0]]
        else:
            summed = y_ref[f, first:first + count, 0].astype(jnp.float32)
            for k in range(1, blocks):
                summed = summed + y_ref[f, first:first + count, k].astype(jnp.float32)
            parts = split(summed)
        smoothed = None
        for part in parts:
            part = part.reshape(many, cols)
            left = jnp.concatenate([part[:, :sources], part[:, sources:]], axis=0)
            term = matmul(jnp.concatenate([left, left], axis=1), smooth_ref[...])
            smoothed = term if smoothed is None else smoothed + term
        real_y, imag_y = smoothed[:many], smoothed[many:]
        cos_g = cos_g_ref[f, first:first + count].reshape(many, 1)
        sin_g = sin_g_ref[f, first:first + count].reshape(many, 1)
        shape = (count, receivers, sources)
        mix_ref[f, 0, first:first + count] = (cos_g * real_y - sin_g * imag_y).reshape(shape)
        mix_ref[f, 1, first:first + count] = (sin_g * real_y + cos_g * imag_y).reshape(shape)


def gate_kernel(y_ref, cos_g_ref, sin_g_ref, smooth_ref, wave_ref, out_ref, mix_ref):
    rows, receivers, gate_len, sources = out_ref.shape
    freq_count, all_rows = y_ref.shape[:2]
    high = 16

    for first in range(0, all_rows, 4):

        @pl.when(pl.program_id(0) * rows == first)
        def _():
            mix_rows(y_ref, cos_g_ref, sin_g_ref, smooth_ref, mix_ref, first, 4)

    for i in range(rows):
        row = pl.program_id(0) * rows + i
        for r in range(receivers):
            mixed = [
                [
                    jnp.broadcast_to(mix_ref[f, p, row, r:r + 1], (high, sources)).astype(
                        jnp.bfloat16
                    )
                    for p in range(2)
                ]
                for f in range(freq_count)
            ]
            for top in range(0, gate_len, high):
                down = slice(top, top + high)
                terms = [
                    wave_ref[f, 0, down] * mixed[f][0] - wave_ref[f, 1, down] * mixed[f][1]
                    for f in range(freq_count)
                ]
                total = terms[0]
                if freq_count > 1:
                    total = sum(term.astype(jnp.float32) for term in terms)
                out_ref[i, r, down] = total.astype(out_ref.dtype)


def gate(arrived, cos_g, sin_g, smooth, wave, step):
    freq_count, rows, _, receivers, cols = arrived.shape
    sources = cols // 2
    gate_len = wave.shape[2]
    return pl.pallas_call(
        gate_kernel,
        out_shape=jax.ShapeDtypeStruct((rows, receivers, gate_len, sources), jnp.bfloat16),
        grid=(rows // step,),
        in_specs=[pl.BlockSpec(memory_space=pltpu.VMEM)] * 5,
        out_specs=pl.BlockSpec((step, receivers, gate_len, sources), lambda i: (i, 0, 0, 0)),
        scratch_shapes=[pltpu.VMEM((freq_count, 2, rows, receivers, sources), jnp.float32)],
        compiler_params=pltpu.CompilerParams(vmem_limit_bytes=32 * 2**20),
        name="gate",
    )(arrived, cos_g, sin_g, smooth, wave)


def waves(times, bins):
    phases = bins.reshape((-1,) + (1,) * times.ndim) * times[None] % NT
    angles = phases.astype(jnp.float32) * (2.0 * math.pi / NT)
    return jnp.cos(angles), jnp.sin(angles)


def gate_waves(bins, lanes):
    both = jnp.stack(waves(jnp.arange(GT, dtype=jnp.int32), bins), axis=1).astype(jnp.bfloat16)
    return jnp.broadcast_to(both[..., None], both.shape + (lanes,))


def on_device(src_slots, v_tiles, u_tiles, ranks, col_map, gate_start):
    devices = lax.axis_size("tile")
    freq_count = devices // TC
    blocks_per = devices // TR
    rank_block = RMAX // blocks_per
    turned = rank_block == RMAX
    cols = src_slots.shape[-1]
    tile_len = v_tiles.shape[2]
    receivers = tile_len // devices
    freq_ids = jnp.arange(freq_count, dtype=jnp.int32)

    if turned:
        partial_value = exchange(ranks, col_map, v_tiles, src_slots, u_tiles)
    else:
        outgoing = project(ranks, col_map, v_tiles, src_slots, 4, turned)
        outgoing = outgoing.reshape(devices, rank_block, cols)
        incoming = lax.all_to_all(outgoing, "tile", split_axis=0, concat_axis=0, tiled=True)
        partial_value = expand(col_map, incoming, u_tiles, cols, turned)
    spread = partial_value.reshape(freq_count, devices, receivers, cols)
    arrived = lax.all_to_all(spread, "tile", split_axis=1, concat_axis=1, tiled=True)
    arrived = arrived.reshape(freq_count, TR, blocks_per, receivers, cols)

    bins = 4 + freq_ids * (NT // (2 * freq_count))
    scale = 2.0 / math.sqrt(freq_count)
    cos_g, sin_g = waves(gate_start, bins)
    cos_g, sin_g = scale * cos_g[..., None], scale * sin_g[..., None]
    wave = gate_waves(bins, cols // 2)
    return gate(arrived, cos_g, sin_g, smoother(cols // 2), wave, 4)


def solution(mesh):
    placed = (
        P(("parts", "tile"), None, None),
        P(("parts", "tile"), None, None, None),
        P(("parts", "tile"), None, None, None),
        P("parts", None, None),
        P("parts", None),
        P("parts", "tile"),
    )
    return jax.shard_map(
        on_device,
        mesh=mesh,
        in_specs=placed,
        out_specs=P("parts", "tile", None, None),
        check_vma=False,
    )
```

```python
import functools
import math

import jax
import jax.numpy as jnp
from jax import lax
from jax.experimental import pallas as pl
from jax.experimental.pallas import tpu as pltpu
from jax.sharding import PartitionSpec as P


TC = 16
TR = 16
RMAX = 128
SIDE = 16
NT = 1024
GT = 64
slots = 4


edge_weight = 0.15
centre_weight = 0.7


def matmul(left, right, left_dim=1):
    return lax.dot_general(
        left, right, (((left_dim,), (0,)), ((), ())), preferred_element_type=jnp.float32
    )


def project_kernel(turned, rank_ref, col_ref, v_ref, x_ref, z_ref, left_ref):
    tiles, tile_len, _ = v_ref.shape
    sources = x_ref.shape[-1] // 2
    device = lax.axis_index("tile")
    freq, slot = device // TC, device % TC
    column = col_ref[freq, slot]

    @pl.when(pl.program_id(0) == 0)
    def _():
        real_x = x_ref[0, :, :sources].T
        imag_x = x_ref[0, :, sources:].T
        left_ref[:sources, :tile_len] = real_x
        left_ref[:sources, tile_len:] = -imag_x
        left_ref[sources:, :tile_len] = imag_x
        left_ref[sources:, tile_len:] = real_x

    first = pl.program_id(0) * tiles
    lane = lax.broadcasted_iota(jnp.int32, (1, 2 * RMAX), 1)
    for t in range(0, tiles, 2):
        one, two = v_ref[t], v_ref[t + 1]
        real_v = jnp.concatenate([one[:, :RMAX], two[:, :RMAX]], axis=1)
        imag_v = jnp.concatenate([one[:, RMAX:], two[:, RMAX:]], axis=1)
        both = matmul(left_ref[...], jnp.concatenate([real_v, imag_v], axis=0))
        rank_one = rank_ref[freq, first + t, column]
        rank_two = rank_ref[freq, first + t + 1, column] + RMAX
        live = (lane < rank_one) | ((lane >= RMAX) & (lane < rank_two))
        both = jnp.where(live, both, 0.0).astype(jnp.bfloat16)
        for side in range(2):
            z = both[:, side * RMAX:(side + 1) * RMAX]
            z_ref[t + side] = z if turned else z.T


def project(ranks, col_map, v_tiles, src_slots, tiles, turned):
    _, rows, tile_len, wide = v_tiles.shape
    cols = src_slots.shape[-1]
    shape = (cols, RMAX) if turned else (RMAX, cols)
    return pl.pallas_call(
        lambda *refs: project_kernel(turned, *refs),
        out_shape=jax.ShapeDtypeStruct((rows,) + shape, jnp.bfloat16),
        grid=(rows // tiles,),
        in_specs=[
            pl.BlockSpec(memory_space=pltpu.SMEM),
            pl.BlockSpec(memory_space=pltpu.SMEM),
            pl.BlockSpec((None, tiles, tile_len, wide), lambda i: (0, i, 0, 0)),
            pl.BlockSpec((1, tile_len, cols), lambda i: (0, 0, 0)),
        ],
        out_specs=pl.BlockSpec((tiles,) + shape, lambda i: (i, 0, 0)),
        scratch_shapes=[pltpu.VMEM((cols, 2 * tile_len), jnp.bfloat16)],
        name="project",
    )(ranks, col_map, v_tiles, src_slots)


def expand_kernel(turned, col_ref, z_ref, u_ref, y_ref, acc_ref):
    freq_count = u_ref.shape[0]
    sources = y_ref.shape[-1] // 2
    for f in range(freq_count):
        for x in range(TC):
            z = z_ref[f, x]
            if turned:
                real_z, imag_z = z[:sources], z[sources:]
                upper = jnp.concatenate([real_z, -imag_z], axis=1)
                lower = jnp.concatenate([imag_z, real_z], axis=1)
                left = jnp.concatenate([upper, lower], axis=0)
            else:
                real_z, imag_z = z[:, :sources], z[:, sources:]
                upper = jnp.concatenate([real_z, imag_z], axis=1)
                lower = jnp.concatenate([-imag_z, real_z], axis=1)
                left = jnp.concatenate([upper, lower], axis=0)
            term = matmul(left, u_ref[f, col_ref[f, x]], 1 if turned else 0)
            if x == 0:
                acc_ref[...] = term
            else:
                acc_ref[...] += term
        y_ref[f] = acc_ref[...].astype(jnp.bfloat16).T


def expand(col_map, incoming, u_tiles, cols, turned):
    freq_count = col_map.shape[0]
    rank_block = incoming.shape[-1] if turned else incoming.shape[-2]
    tile_len = u_tiles.shape[-1]
    incoming = incoming.reshape((freq_count, TC) + incoming.shape[1:])
    weights = u_tiles.reshape(freq_count, TC, 2 * rank_block, tile_len)
    return pl.pallas_call(
        lambda *refs: expand_kernel(turned, *refs),
        out_shape=jax.ShapeDtypeStruct((freq_count, tile_len, cols), jnp.bfloat16),
        in_specs=[
            pl.BlockSpec(memory_space=pltpu.SMEM),
            pl.BlockSpec(memory_space=pltpu.VMEM),
            pl.BlockSpec(memory_space=pltpu.VMEM),
        ],
        out_specs=pl.BlockSpec(memory_space=pltpu.VMEM),
        scratch_shapes=[pltpu.VMEM((cols, tile_len), jnp.float32)],
        compiler_params=pltpu.CompilerParams(vmem_limit_bytes=24 * 2**20),
        name="expand",
    )(col_map, incoming, weights)


def far_first(devices):
    return sorted(range(1, devices), key=lambda k: (-(k >> 2), k)) + [0]


def build_left(x, left_ref):
    tile_len, cols = x.shape
    sources = cols // 2
    real_x = x[:, :sources].T
    imag_x = x[:, sources:].T
    left_ref[:sources, :tile_len] = real_x
    left_ref[:sources, tile_len:] = -imag_x
    left_ref[sources:, :tile_len] = imag_x
    left_ref[sources:, tile_len:] = real_x


def project_two(left_ref, tiles, ranks):
    lane = lax.broadcasted_iota(jnp.int32, (1, 2 * RMAX), 1)
    one, two = tiles
    real_v = jnp.concatenate([one[:, :RMAX], two[:, :RMAX]], axis=1)
    imag_v = jnp.concatenate([one[:, RMAX:], two[:, RMAX:]], axis=1)
    both = matmul(left_ref[...], jnp.concatenate([real_v, imag_v], axis=0))
    live = (lane < ranks[0]) | ((lane >= RMAX) & (lane < ranks[1] + RMAX))
    both = jnp.where(live, both, 0.0)
    sources = both.shape[0] // 2
    half = RMAX // 2
    low_lane = lax.broadcasted_iota(jnp.int32, (1, RMAX), 1) < half
    out = []
    for side in range(2):
        real_z = both[:sources, side * RMAX:(side + 1) * RMAX]
        imag_z = both[sources:, side * RMAX:(side + 1) * RMAX]
        lower = jnp.where(low_lane, real_z, pltpu.roll(imag_z, half, axis=1))
        upper = jnp.where(low_lane, pltpu.roll(real_z, half, axis=1), imag_z)
        out.append((lower.astype(jnp.bfloat16), upper.astype(jnp.bfloat16)))
    return out


def fetch_tiles(v_hbm, tile_ref, sems, rows):
    copies = [
        pltpu.make_async_copy(v_hbm.at[0, row], tile_ref.at[n], sems.at[n])
        for n, row in enumerate(rows)
    ]
    for copy in copies:
        copy.start()
    return copies


def project_all(copies, left_ref, tile_ref, ranks):
    out = []
    for n in range(0, len(copies), 2):
        copies[n].wait()
        copies[n + 1].wait()
        out += project_two(left_ref, [tile_ref[n], tile_ref[n + 1]], ranks[n:n + 2])
    return out


def project_rows(left_ref, v_ref, rows, ranks):
    out = []
    for n in range(0, len(rows), 2):
        tiles = [v_ref[0, rows[n]], v_ref[0, rows[n + 1]]]
        out += project_two(left_ref, tiles, ranks[n:n + 2])
    return out


def send_first_kernel(ids, rank_hbm, col_hbm, v_hbm, x_hbm, *refs):
    count = len(ids)
    low_refs = refs[:count]
    left_ref, tile_ref, sems, x_ref, rank_ref, col_ref, more_sems = refs[count:]
    device = lax.axis_index("tile")
    rows = [jnp.bitwise_xor(device, k) for k in ids]
    more = [
        pltpu.make_async_copy(x_hbm.at[0], x_ref, more_sems.at[0]),
        pltpu.make_async_copy(rank_hbm.at[0], rank_ref, more_sems.at[1]),
        pltpu.make_async_copy(col_hbm, col_ref, more_sems.at[2]),
    ]
    for copy in more:
        copy.start()
    copies = fetch_tiles(v_hbm, tile_ref, sems, rows)
    more[0].wait()
    build_left(x_ref[...], left_ref)
    more[1].wait()
    more[2].wait()
    column = col_ref[0, device]
    ranks = [rank_ref[row, column] for row in rows]
    for n, (lower, _) in enumerate(project_all(copies, left_ref, tile_ref, ranks)):
        low_refs[n][...] = lower


def send_far_kernel(skip, ids, rank_ref, col_ref, x_ref, v_ref, *refs):
    count = len(ids)
    low_refs, refs = refs[:count - skip], refs[count - skip:]
    slot_ref, left_ref, up_ref = refs
    device = lax.axis_index("tile")
    column = col_ref[0, device]
    sources = x_ref.shape[-1] // 2
    rows = [jnp.bitwise_xor(device, k) for k in ids]
    ranks = [rank_ref[0, row, column] for row in rows]
    build_left(x_ref[0], left_ref)
    for n, (lower, upper) in enumerate(project_rows(left_ref, v_ref, rows, ranks)):
        if n >= skip:
            low_refs[n - skip][...] = lower
        up_ref[n] = upper
    found = [jnp.int32(0)] * slots
    used = jnp.int32(0)
    for n, rank in enumerate(ranks):
        heavy = rank > RMAX // 2
        found = [jnp.where(heavy & (used == c), n, found[c]) for c in range(slots)]
        used = used + heavy.astype(jnp.int32)
    for c in range(slots):
        tile = up_ref[found[c]]
        slot_ref[c * sources:(c + 1) * sources] = jnp.where(
            c < used, tile, jnp.zeros_like(tile)
        )


def send_near_kernel(ids, rank_ref, col_ref, x_ref, v_ref, *refs):
    z_refs, left_ref = refs[:-1], refs[-1]
    device = lax.axis_index("tile")
    column = col_ref[0, device]
    rows = [jnp.bitwise_xor(device, k) for k in ids]
    ranks = [rank_ref[0, row, column] for row in rows]
    sources = x_ref.shape[-1] // 2
    build_left(x_ref[0], left_ref)
    for n, (lower, upper) in enumerate(project_rows(left_ref, v_ref, rows, ranks)):
        z_refs[n][:sources] = lower
        z_refs[n][sources:] = upper


def hand_on_kernel(far, half, rank_ref, col_ref, slot_ref, *out_refs):
    device = lax.axis_index("tile")
    origin = jnp.bitwise_xor(device, half)
    column = col_ref[0, origin]
    sources = out_refs[0].shape[0]
    used = jnp.int32(0)
    for k in far:
        heavy = rank_ref[0, jnp.bitwise_xor(origin, k), column] > RMAX // 2
        held = heavy & (used < slots)
        at = pl.multiple_of(jnp.minimum(used, slots - 1) * sources, sources)
        tile = slot_ref[pl.ds(at, sources)]
        out_refs[k - half][...] = jnp.where(held, tile, jnp.zeros_like(tile))
        used = used + heavy.astype(jnp.int32)


def specs():
    return (
        pl.BlockSpec(memory_space=m) for m in (pltpu.VMEM, pltpu.SMEM, pltpu.HBM)
    )


def send_cost(count, v_tiles, cols):
    tile_len, wide = v_tiles.shape[2:]
    return pl.CostEstimate(
        flops=4 * count * cols * tile_len * RMAX,
        bytes_accessed=count * tile_len * wide * 2,
        transcendentals=0,
    )


def tile_scratch(count, v_tiles, cols):
    tile_len, wide = v_tiles.shape[2:]
    return [
        pltpu.VMEM((cols, 2 * tile_len), jnp.bfloat16),
        pltpu.VMEM((count, tile_len, wide), jnp.bfloat16),
        pltpu.SemaphoreType.DMA((count,)),
    ]


def send_first(ids, ranks, col_map, v_tiles, src_slots):
    cols = src_slots.shape[-1]
    count = len(ids)
    vmem, _, hbm = specs()
    return pl.pallas_call(
        functools.partial(send_first_kernel, ids),
        out_shape=[jax.ShapeDtypeStruct((cols // 2, RMAX), jnp.bfloat16)] * count,
        in_specs=[hbm] * 4,
        out_specs=[vmem] * count,
        scratch_shapes=tile_scratch(count, v_tiles, cols)
        + [
            pltpu.VMEM(src_slots.shape[1:], jnp.bfloat16),
            pltpu.SMEM(ranks.shape[1:], jnp.int32),
            pltpu.SMEM(col_map.shape, jnp.int32),
            pltpu.SemaphoreType.DMA((3,)),
        ],
        compiler_params=pltpu.CompilerParams(vmem_limit_bytes=60 * 2**20),
        cost_estimate=send_cost(count, v_tiles, cols),
        name="send_first",
    )(ranks, col_map, v_tiles, src_slots)


def send_far(skip, ids, ranks, col_map, v_tiles, src_slots):
    cols = src_slots.shape[-1]
    count = len(ids)
    vmem, smem, _ = specs()
    shapes = [jax.ShapeDtypeStruct((cols // 2, RMAX), jnp.bfloat16)] * (count - skip)
    shapes.append(jax.ShapeDtypeStruct((slots * cols // 2, RMAX), jnp.bfloat16))
    out = pl.pallas_call(
        functools.partial(send_far_kernel, skip, ids),
        out_shape=shapes,
        in_specs=[smem, smem, vmem, vmem],
        out_specs=[vmem] * len(shapes),
        scratch_shapes=tile_scratch(count, v_tiles, cols)[:1]
        + [pltpu.VMEM((count, cols // 2, RMAX), jnp.bfloat16)],
        compiler_params=pltpu.CompilerParams(vmem_limit_bytes=12 * 2**20),
        cost_estimate=send_cost(count, v_tiles, cols),
        name="send_far",
    )(ranks, col_map, src_slots, v_tiles)
    return out[:-1], out[-1]


def send_near(ids, ranks, col_map, v_tiles, src_slots):
    cols = src_slots.shape[-1]
    count = len(ids)
    vmem, smem, _ = specs()
    return pl.pallas_call(
        functools.partial(send_near_kernel, ids),
        out_shape=[jax.ShapeDtypeStruct((cols, RMAX), jnp.bfloat16)] * count,
        in_specs=[smem, smem, vmem, vmem],
        out_specs=[vmem] * count,
        scratch_shapes=tile_scratch(count, v_tiles, cols)[:1],
        compiler_params=pltpu.CompilerParams(vmem_limit_bytes=12 * 2**20),
        cost_estimate=send_cost(count, v_tiles, cols),
        name="send_near",
    )(ranks, col_map, src_slots, v_tiles)


def hand_on(far, half, ranks, col_map, held):
    vmem, smem, _ = specs()
    shape = (held.shape[0] // slots, RMAX)
    return pl.pallas_call(
        functools.partial(hand_on_kernel, far, half),
        out_shape=[jax.ShapeDtypeStruct(shape, jnp.bfloat16)] * half,
        in_specs=[smem, smem, vmem],
        out_specs=[vmem] * half,
        compiler_params=pltpu.CompilerParams(vmem_limit_bytes=4 * 2**20),
        cost_estimate=pl.CostEstimate(
            flops=0, bytes_accessed=2 * half * shape[0] * RMAX * 2, transcendentals=0
        ),
        name="hand_on",
    )(ranks, col_map, held)


def add_kernel(lows, ups, first, last, rank_ref, col_ref, u_hbm, *refs):
    count = len(lows) + len(ups)
    z_refs, out_ref = refs[:count], refs[count if first else count + 1]
    total_ref, low_ref, up_ref, sems = refs[-4:]
    sources = total_ref.shape[0]
    tile_len = u_hbm.shape[-1]
    device = lax.axis_index("tile")
    half = RMAX // 2

    def fetches(n, where, held_ref):
        k, side, _ = where
        column = col_ref[0, jnp.bitwise_xor(device, k)]
        at = n if held_ref is low_ref else n + len(lows)
        return [
            pltpu.make_async_copy(
                u_hbm.at[0, column, pl.ds(part * RMAX + side * half, half)],
                held_ref.at[n, pl.ds(part * half, half)],
                sems.at[at, part],
            )
            for part in range(2)
        ]

    def add(items, start):
        left, real_w, imag_w = [], [], []
        for z_ref, held_ref, n, (_, _, offset) in items:
            real_u, imag_u = held_ref[n, :half], held_ref[n, half:]
            left.append(z_ref[offset * sources:(offset + 1) * sources])
            real_w += [real_u, -imag_u]
            imag_w += [imag_u, real_u]
        left = jnp.concatenate(left, axis=1)
        for part, weights in enumerate((real_w, imag_w)):
            at = slice(part * tile_len, (part + 1) * tile_len)
            term = matmul(left, jnp.concatenate(weights, axis=0))
            if start is None:
                total_ref[:, at] = term
            else:
                total_ref[:, at] = start[:, at] + term

    low_copies = [fetches(n, where, low_ref) for n, where in enumerate(lows)]
    up_copies = [fetches(n, where, up_ref) for n, where in enumerate(ups)]
    alive = [
        rank_ref[0, device, col_ref[0, jnp.bitwise_xor(device, where[0])]] > half
        for where in ups
    ]
    for copies in low_copies:
        for copy in copies:
            copy.start()
    for copies, live in zip(up_copies, alive):

        @pl.when(live)
        def _():
            for copy in copies:
                copy.start()

    items = [(z, low_ref, n, at) for n, (z, at) in enumerate(zip(z_refs, lows))]
    for n in range(0, len(lows), 2):
        for copy in low_copies[n] + low_copies[n + 1]:
            copy.wait()
        begin = (None if first else refs[count]) if n == 0 else total_ref
        add(items[n:n + 2], begin)
    for n, (z_ref, where) in enumerate(zip(z_refs[len(lows):], ups)):

        @pl.when(alive[n])
        def _():
            for copy in up_copies[n]:
                copy.wait()
            add([(z_ref, up_ref, n, where)], total_ref)

    if last:
        total = total_ref[...].astype(jnp.bfloat16)
        out_ref[0, :, :sources] = total[:, :tile_len].T
        out_ref[0, :, sources:] = total[:, tile_len:].T
    else:
        out_ref[...] = total_ref[...]


def add_tiles(lows, ups, ranks, col_map, u_tiles, sources, total=None, last=False):
    first = total is None
    tile_len = u_tiles.shape[-1]
    vmem, smem, hbm = specs()
    tiles = [tile for tile, _ in lows + ups]
    operands = [ranks, col_map, u_tiles, *tiles] + ([] if first else [total])
    shape = (
        jax.ShapeDtypeStruct((1, tile_len, 2 * sources), jnp.bfloat16)
        if last
        else jax.ShapeDtypeStruct((sources, 2 * tile_len), jnp.float32)
    )
    kernel = functools.partial(
        add_kernel, [at for _, at in lows], [at for _, at in ups], first, last
    )
    return pl.pallas_call(
        kernel,
        out_shape=shape,
        in_specs=[smem, smem, hbm] + [vmem] * (len(operands) - 3),
        out_specs=vmem,
        scratch_shapes=[
            pltpu.VMEM((sources, 2 * tile_len), jnp.float32),
            pltpu.VMEM((len(lows), RMAX, tile_len), jnp.bfloat16),
            pltpu.VMEM((len(ups), RMAX, tile_len), jnp.bfloat16),
            pltpu.SemaphoreType.DMA((len(tiles), 2)),
        ],
        compiler_params=pltpu.CompilerParams(vmem_limit_bytes=12 * 2**20),
        cost_estimate=pl.CostEstimate(
            flops=4 * len(tiles) * sources * RMAX * tile_len,
            bytes_accessed=len(tiles) * sources * RMAX * 2,
            transcendentals=0,
        ),
        name="add_tiles",
    )(*operands)


def exchange(ranks, col_map, v_tiles, src_slots, u_tiles):
    devices = lax.axis_size("tile")
    half = devices // 2
    sources = src_slots.shape[-1] // 2
    order = far_first(devices)
    far, near = order[:half], order[half:]
    begin, rest = far[:2], far[2:]

    def swap(value, k):
        return lax.ppermute(value, "tile", [(d, d ^ k) for d in range(devices)])

    lower = send_first(begin, ranks, col_map, v_tiles, src_slots)
    arrived = {k: swap(tile, k) for k, tile in zip(begin, lower)}
    lower, held = send_far(len(begin), far, ranks, col_map, v_tiles, src_slots)
    held = swap(held, half)
    whole = send_near(near, ranks, col_map, v_tiles, src_slots)
    arrived.update((k, swap(tile, k) if k else tile) for k, tile in zip(near, whole))
    arrived.update((k, swap(tile, k)) for k, tile in zip(rest, lower))
    handed = hand_on(far, half, ranks, col_map, held)
    uppers = {k: swap(handed[k], k) if k else handed[k] for k in near}

    own = sorted(near)
    groups = [
        (
            [(arrived[k], (k, 0, 0)) for k in own],
            [(arrived[k], (k, 1, 1)) for k in own],
        ),
        (
            [(arrived[k], (k, 0, 0)) for k in far],
            [(uppers[k], (k + half, 1, 0)) for k in own],
        ),
    ]
    total = None
    for n, (lows, ups) in enumerate(groups):
        last = n == len(groups) - 1
        total = add_tiles(lows, ups, ranks, col_map, u_tiles, sources, total, last)
        if n == 0:
            late = total
    return total, late


def too_many(ranks, col_map, devices):
    ids = jnp.arange(devices, dtype=jnp.int32)
    mine = (col_map[0][:, None] == ids[None, :]).astype(jnp.int32)
    heavy = (ranks[0] > RMAX // 2).astype(jnp.int32)
    far = ((ids[:, None] ^ ids[None, :]) >= devices // 2).astype(jnp.int32)
    by_slot = jnp.sum(mine[:, None, :] * heavy[None, :, :], axis=-1)
    return jnp.any(jnp.sum(by_slot * far, axis=1) > slots)


def split(value):
    high = value.astype(jnp.bfloat16)
    return high, (value - high.astype(jnp.float32)).astype(jnp.bfloat16)


def smoother(sources):
    place = jnp.arange(sources, dtype=jnp.int32)
    row, column = place // SIDE, place % SIDE

    def one(at):
        apart = jnp.abs(at[:, None] - at[None, :])
        return jnp.where(apart == 0, centre_weight, jnp.where(apart == 1, edge_weight, 0.0))

    return jnp.concatenate(split(one(row) * one(column)), axis=0)


def mix_rows(y_ref, cos_g_ref, sin_g_ref, smooth_ref, mix_ref, first, count):
    freq_count, _, blocks, receivers, cols = y_ref.shape
    sources = cols // 2
    many = count * receivers
    for f in range(freq_count):
        if blocks == 1:
            parts = [y_ref[f, first:first + count, 0]]
        else:
            summed = y_ref[f, first:first + count, 0].astype(jnp.float32)
            for k in range(1, blocks):
                summed = summed + y_ref[f, first:first + count, k].astype(jnp.float32)
            parts = split(summed)
        smoothed = None
        for part in parts:
            part = part.reshape(many, cols)
            left = jnp.concatenate([part[:, :sources], part[:, sources:]], axis=0)
            term = matmul(jnp.concatenate([left, left], axis=1), smooth_ref[...])
            smoothed = term if smoothed is None else smoothed + term
        real_y, imag_y = smoothed[:many], smoothed[many:]
        cos_g = cos_g_ref[f, first:first + count].reshape(many, 1)
        sin_g = sin_g_ref[f, first:first + count].reshape(many, 1)
        shape = (count, receivers, sources)
        mix_ref[f, 0, first:first + count] = (cos_g * real_y - sin_g * imag_y).reshape(shape)
        mix_ref[f, 1, first:first + count] = (sin_g * real_y + cos_g * imag_y).reshape(shape)


def gate_kernel(y_ref, cos_g_ref, sin_g_ref, smooth_ref, wave_ref, out_ref, mix_ref):
    rows, receivers, gate_len, sources = out_ref.shape
    freq_count, all_rows = y_ref.shape[:2]
    high = 16

    for first in range(0, all_rows, 4):

        @pl.when(pl.program_id(0) * rows == first)
        def _():
            mix_rows(y_ref, cos_g_ref, sin_g_ref, smooth_ref, mix_ref, first, 4)

    for i in range(rows):
        row = pl.program_id(0) * rows + i
        for r in range(receivers):
            mixed = [
                [
                    jnp.broadcast_to(mix_ref[f, p, row, r:r + 1], (high, sources)).astype(
                        jnp.bfloat16
                    )
                    for p in range(2)
                ]
                for f in range(freq_count)
            ]
            for top in range(0, gate_len, high):
                down = slice(top, top + high)
                terms = [
                    wave_ref[f, 0, down] * mixed[f][0] - wave_ref[f, 1, down] * mixed[f][1]
                    for f in range(freq_count)
                ]
                total = terms[0]
                if freq_count > 1:
                    total = sum(term.astype(jnp.float32) for term in terms)
                out_ref[i, r, down] = total.astype(out_ref.dtype)


def gate(arrived, cos_g, sin_g, smooth, wave, step):
    freq_count, rows, _, receivers, cols = arrived.shape
    sources = cols // 2
    gate_len = wave.shape[2]
    return pl.pallas_call(
        gate_kernel,
        out_shape=jax.ShapeDtypeStruct((rows, receivers, gate_len, sources), jnp.bfloat16),
        grid=(rows // step,),
        in_specs=[pl.BlockSpec(memory_space=pltpu.VMEM)] * 5,
        out_specs=pl.BlockSpec((step, receivers, gate_len, sources), lambda i: (i, 0, 0, 0)),
        scratch_shapes=[pltpu.VMEM((freq_count, 2, rows, receivers, sources), jnp.float32)],
        compiler_params=pltpu.CompilerParams(vmem_limit_bytes=32 * 2**20),
        name="gate",
    )(arrived, cos_g, sin_g, smooth, wave)


def waves(times, bins):
    phases = bins.reshape((-1,) + (1,) * times.ndim) * times[None] % NT
    angles = phases.astype(jnp.float32) * (2.0 * math.pi / NT)
    return jnp.cos(angles), jnp.sin(angles)


def gate_waves(bins, lanes):
    both = jnp.stack(waves(jnp.arange(GT, dtype=jnp.int32), bins), axis=1).astype(jnp.bfloat16)
    return jnp.broadcast_to(both[..., None], both.shape + (lanes,))


def on_device(src_slots, v_tiles, u_tiles, ranks, col_map, gate_start):
    devices = lax.axis_size("tile")
    freq_count = devices // TC
    blocks_per = devices // TR
    rank_block = RMAX // blocks_per
    turned = rank_block == RMAX
    cols = src_slots.shape[-1]
    tile_len = v_tiles.shape[2]
    receivers = tile_len // devices
    freq_ids = jnp.arange(freq_count, dtype=jnp.int32)

    def all_at_once():
        outgoing = project(ranks, col_map, v_tiles, src_slots, 4, turned)
        if not turned:
            outgoing = outgoing.reshape(devices, rank_block, cols)
        incoming = lax.all_to_all(outgoing, "tile", split_axis=0, concat_axis=0, tiled=True)
        return expand(col_map, incoming, u_tiles, cols, turned)

    if turned:
        partial_value, late = exchange(ranks, col_map, v_tiles, src_slots, u_tiles)
        late_ranks, _ = lax.optimization_barrier((ranks, late[:8, :128]))
        partial_value = lax.cond(
            too_many(late_ranks, col_map, devices),
            lambda _: all_at_once(),
            lambda kept: kept,
            partial_value,
        )
    else:
        partial_value = all_at_once()
    spread = partial_value.reshape(freq_count, devices, receivers, cols)
    arrived = lax.all_to_all(spread, "tile", split_axis=1, concat_axis=1, tiled=True)
    arrived = arrived.reshape(freq_count, TR, blocks_per, receivers, cols)

    bins = 4 + freq_ids * (NT // (2 * freq_count))
    scale = 2.0 / math.sqrt(freq_count)
    cos_g, sin_g = waves(gate_start, bins)
    cos_g, sin_g = scale * cos_g[..., None], scale * sin_g[..., None]
    wave = gate_waves(bins, cols // 2)
    return gate(arrived, cos_g, sin_g, smoother(cols // 2), wave, 4)


def solution(mesh):
    placed = (
        P(("parts", "tile"), None, None),
        P(("parts", "tile"), None, None, None),
        P(("parts", "tile"), None, None, None),
        P("parts", None, None),
        P("parts", None),
        P("parts", "tile"),
    )
    return jax.shard_map(
        on_device,
        mesh=mesh,
        in_specs=placed,
        out_specs=P("parts", "tile", None, None),
        check_vma=False,
    )
```
